32 devices in a mesh: head: 2 (over y), key: 4 (over z), hid: 4 (over x, core).
Axes of the slice: x: 2, y: 2, z: 4, core: 2. Of those that a mesh axis runs over, the one named last changes fastest.
Arguments:
- tokens: bfloat16 [1024, 8192], P('key', 'hid'), may hold values from -6 to 6
- query_weight: bfloat16 [8192, 8192], P('hid', 'head'), may hold values from -0.0625 to 0.0625
- key_weight: bfloat16 [8192, 1024], P('hid', 'head'), may hold values from -0.0625 to 0.0625
- value_weight: bfloat16 [8192, 1024], P('hid', 'head'), may hold values from -0.0625 to 0.0625
- output_weight: bfloat16 [8192, 8192], P(('head', 'hid')), may hold values from -0.09375 to 0.09375
- key_cache: bfloat16 [8192, 8, 128], P('key', 'head'), may hold values from -2000 to 2000
- value_cache: bfloat16 [8192, 8, 128], P('key', 'head'), may hold values from -6 to 6
- cache_places: int32 [32], P('key'), may hold values from 1 to 510, as said below
- slab_places: int32 [4], replicated, may hold values from 0 to 511, as said below
Outputs:
- attended: bfloat16 [1024, 8192], P('key', ('head', 'hid'))
The draws below stay inside these ranges and needn't reach their ends.
Inputs may be any that keep to these rules, and one draw needn't show every extreme that they name: The 32 entries of cache_places and the 4 entries of slab_places are all different from one another. `slab_places`: see cache_places: no slab shares a block number with another slab or with a resident block.
All inputs are finite; a program needn't handle non-finite values.
Results may differ from the reference program's by a relative error of at most 0.039.
Values may be sent and summed in bfloat16 or wider, within the bound.
A program may use at most 192 MiB of HBM per device.

```python
import math
import jax
import jax.numpy as jnp
from jax import lax

D = 8192
H = 64
KVH = 8
HD = 128
SEQ = 131072
TOK_DEV = 256
NSLAB = 4
NQ = 1024
NKB = 32
NK = 8192


def block_spots(key):
    blocks = SEQ // TOK_DEV
    middle = 2 + jax.random.permutation(jax.random.fold_in(key, 11), blocks - 4).astype(jnp.int32)
    cache_part = jnp.concatenate([jnp.array([1, blocks - 2], jnp.int32), middle[:NKB - 2]])
    slab_part = jnp.concatenate([jnp.array([0, blocks - 1], jnp.int32), middle[NKB - 2:NKB - 4 + NSLAB]])
    cache_order = jax.random.permutation(jax.random.fold_in(key, 13), NKB)
    slab_order = jax.random.permutation(jax.random.fold_in(key, 17), NSLAB)
    return (cache_part[cache_order].astype(jnp.int32), slab_part[slab_order].astype(jnp.int32))


def draw_cache_places(key, part):
    return block_spots(key)[0]


def draw_slab_places(key, part):
    return block_spots(key)[1]


def draw_key_cache(key, part):
    normal_base = jnp.clip(jax.random.normal(jax.random.fold_in(key, 3), (NK, KVH, HD), jnp.float32), -6.0, 6.0)
    result = 2.0 * normal_base
    return result.astype(jnp.bfloat16)


def raised(values, rng, source, target, shards_of, factor):
    def block_of(dim):
        return (jnp.arange(values.shape[dim]) // (values.shape[dim] // shards_of)).reshape((-1,) + (1,) * (values.ndim - 1 - dim))

    one_side = jax.random.permutation(rng, shards_of)[block_of(target)]
    second = (block_of(target) + shards_of // 2) % shards_of
    return jnp.where((block_of(source) == one_side) | (block_of(source) == second), factor * values, values)


def steps_of(own_key, extent, shards, low, largest):
    def one(dim, shards_of):
        steps = jax.random.uniform(jax.random.fold_in(jax.random.fold_in(own_key, 6), dim), (shards_of,), jnp.float32, low / len(shards), largest / len(shards))
        return jnp.repeat(jnp.exp(steps), extent[dim] // shards_of).reshape((-1,) + (1,) * (len(extent) - dim - 1))

    factor_of = one(*shards[0])
    for cut in shards[1:]:
        factor_of = factor_of * one(*cut)
    return factor_of


def gaussian(rng, dims, width, reach, split=(), kind=jnp.bfloat16):
    values = jax.random.normal(rng, dims, jnp.float32) * width
    if len(split) > 0:
        values = steps_of(rng, dims, split, -0.22, 0.18) * values
    return jnp.clip(values, min=-reach, max=reach).astype(kind)


def heavy_noise(own_key, dims, scale, most, cuts, heavy, kind=jnp.bfloat16):
    values = scale * jax.random.normal(own_key, dims, jnp.float32)
    if cuts:
        values = values * steps_of(own_key, dims, cuts, -0.22, 0.18)
    return jnp.clip(raised(values, jax.random.fold_in(own_key, 3), *heavy), -most, most).astype(kind)


def setup_inputs(seed: int = 0) -> dict:
    seeds = jax.random.split(jax.random.key(seed), 10)
    return {
        "tokens": gaussian(seeds[0], (NQ, D), 1.0, 6.0, ((0, 4), (1, 4))),
        "query_weight": gaussian(seeds[1], (D, H * HD), D ** -0.5, 0.0625, ((0, 4), (1, 2))),
        "key_weight": gaussian(seeds[2], (D, KVH * HD), D ** -0.5, 0.0625, ((0, 4), (1, 2))),
        "value_weight": gaussian(seeds[3], (D, KVH * HD), D ** -0.5, 0.0625, ((0, 4), (1, 2))),
        "output_weight": heavy_noise(seeds[4], (H * HD, D), (H * HD) ** -0.5, 0.09375, ((0, 8),), (0, 1, 8, 2.0)),
        "key_cache": draw_key_cache(jax.random.fold_in(seeds[9], 71), 0),
        "value_cache": gaussian(seeds[6], (NK, KVH, HD), 1.0, 6.0, ((0, 4), (1, 2))),
        "cache_places": draw_cache_places(jax.random.fold_in(seeds[9], 71), 0),
        "slab_places": draw_slab_places(jax.random.fold_in(seeds[9], 71), 0),
    }


THETA = 500000.0
NEGATIVE = -1e+30

def rotate(vectors, spots):
    middle = vectors.shape[-1] // 2
    freq_index = jnp.arange(middle, dtype=jnp.float32)
    frequency = jnp.exp(freq_index * (-2.0 * math.log(THETA) / vectors.shape[-1]))
    angles = spots.astype(jnp.float32)[:, None] * frequency[None, :]
    cosine_part = jnp.cos(angles)[:, None, :]
    sine_part = jnp.sin(angles)[:, None, :]
    leading = vectors[..., :middle]
    trailing = vectors[..., middle:]
    return jnp.concatenate([leading * cosine_part - trailing * sine_part, trailing * cosine_part + leading * sine_part], axis=-1)

def reference(tokens, query_weight, key_weight, value_weight, output_weight, key_cache, value_cache, cache_places, slab_places):
    offsets = jnp.arange(TOK_DEV, dtype=jnp.int32)
    query_spots = (slab_places[:, None] * TOK_DEV + offsets[None, :]).reshape(NQ).astype(jnp.int32)
    cache_spots = (cache_places[:, None] * TOK_DEV + offsets[None, :]).reshape(NK).astype(jnp.int32)
    query_raw = jnp.dot(tokens, query_weight, preferred_element_type=jnp.float32).reshape(NQ, H, HD)
    key_raw = jnp.dot(tokens, key_weight, preferred_element_type=jnp.float32).reshape(NQ, KVH, HD)
    value_raw = jnp.dot(tokens, value_weight, preferred_element_type=jnp.float32).reshape(NQ, KVH, HD)
    group_heads = H // KVH
    queries = rotate(query_raw, query_spots).astype(jnp.bfloat16).reshape(NQ, KVH, group_heads, HD)
    keys_new = rotate(key_raw, query_spots).astype(jnp.bfloat16)
    values_new = value_raw.astype(jnp.bfloat16)
    key_rows = jnp.concatenate([key_cache, keys_new], axis=0)
    value_rows = jnp.concatenate([value_cache, values_new], axis=0)
    key_spots = jnp.concatenate([cache_spots, query_spots], axis=0).astype(jnp.int32)
    block_rows = math.gcd(NQ, 512)
    score_scale = 1.0 / math.sqrt(HD)
    query_blocks = jnp.transpose(queries, (1, 0, 2, 3)).reshape(KVH, NQ // block_rows, block_rows, group_heads, HD)
    spot_blocks = query_spots.reshape(NQ // block_rows, block_rows)
    key_heads = jnp.transpose(key_rows, (1, 0, 2))
    value_heads = jnp.transpose(value_rows, (1, 0, 2))

    def head_fn(inputs):
        query_head, key_head, value_head = inputs
        key_float = key_head.astype(jnp.float32)
        value_float = value_head.astype(jnp.float32)

        def block_fn(block_pair):
            query_block, spot_block = block_pair
            scores = jnp.einsum('rgd,cd->rgc', query_block.astype(jnp.float32), key_float) * score_scale
            visible = key_spots[None, None, :] <= spot_block[:, None, None]
            peaks = lax.optimization_barrier(jnp.max(jnp.where(visible, scores, NEGATIVE), axis=-1))
            weights = jnp.where(visible, jnp.exp(scores - peaks[..., None]), 0.0)
            totals = lax.optimization_barrier(jnp.sum(weights, axis=-1))
            rounded = lax.optimization_barrier(weights.astype(jnp.bfloat16)).astype(jnp.float32)
            summed = jnp.einsum('rgc,cd->rgd', rounded, value_float)
            return (summed / totals[..., None]).astype(jnp.bfloat16)
        return lax.map(block_fn, (query_head, spot_blocks))
    heads_all = lax.map(head_fn, (query_blocks, key_heads, value_heads))
    heads_out = jnp.transpose(heads_all, (1, 2, 0, 3, 4)).reshape(NQ, H * HD)
    return jnp.dot(heads_out, output_weight, preferred_element_type=jnp.float32).astype(jnp.bfloat16)
```

```python
import functools
import math

import jax
import jax.numpy as jnp
from jax import lax
from jax.experimental import pallas as pl
from jax.experimental.pallas import tpu as pltpu
from jax.sharding import PartitionSpec as P

H = 64
KVH = 8
THETA = 500000.0
FAR = 1 << 24
BF = jnp.bfloat16
F32 = jnp.float32
LOG2E = 1.4426950408889634


def estimate(flops, size, trans=0):
    return pl.CostEstimate(flops=flops, bytes_accessed=size, transcendentals=trans)


def params():
    return pltpu.CompilerParams(dimension_semantics=("arbitrary",), vmem_limit_bytes=40 << 20)


def project(tokens, wq, wk, wv, dest, group, heads_cols, hd, addends, dtype):
    rows, depth = tokens.shape
    tile = min(512, heads_cols)
    steps = heads_cols // tile
    width = heads_cols + 2 * hd
    count = len(addends)

    def kernel(where_ref, t_ref, q_ref, k_ref, v_ref, *rest):
        adds, out = rest[:count], rest[count]
        j = pl.program_id(0)

        def emit(first, size, w_ref):
            part = jnp.dot(t_ref[...], w_ref[...], preferred_element_type=F32)
            span = pl.ds(first, size)
            for a in adds:
                part = part + a[:, span].astype(F32)
            out[:, span] = part.astype(dtype)

        emit(pl.multiple_of(j * tile, tile), tile, q_ref)

        @pl.when(j == 0)
        def _():
            emit(heads_cols, hd, k_ref)
            emit(heads_cols + hd, hd, v_ref)

    whole = pl.BlockSpec((rows, width), lambda j, w: (0, 0))
    return pl.pallas_call(
        kernel,
        grid_spec=pltpu.PrefetchScalarGridSpec(
            num_scalar_prefetch=1,
            grid=(steps,),
            in_specs=[
                pl.BlockSpec((rows, depth), lambda j, w: (0, 0)),
                pl.BlockSpec((depth, tile), lambda j, w: (0, w[0] * steps + j)),
                pl.BlockSpec((depth, hd), lambda j, w: (0, w[1])),
                pl.BlockSpec((depth, hd), lambda j, w: (0, w[1])),
            ]
            + [whole] * count,
            out_specs=whole,
        ),
        out_shape=jax.ShapeDtypeStruct((rows, width), dtype),
        compiler_params=params(),
        cost_estimate=estimate(2 * rows * depth * width, 2 * depth * width),
        name="project",
    )(jnp.stack([dest, group]).astype(jnp.int32), tokens, wq, wk, wv, *addends)


def turn(summed, cosine, sine, heads_cols):
    rows, width = summed.shape
    hd = cosine.shape[1]

    def kernel(u_ref, c_ref, s_ref, q_ref, kv_ref):
        c = c_ref[...]
        s = s_ref[...]
        for h in range(heads_cols // hd + 1):
            u = u_ref[:, h * hd : (h + 1) * hd]
            r = (u * c + pltpu.roll(u, hd // 2, 1) * s).astype(BF)
            if h < heads_cols // hd:
                q_ref[:, h * hd : (h + 1) * hd] = r
            else:
                kv_ref[:, :hd] = r
        kv_ref[:, hd:] = u_ref[:, heads_cols + hd :].astype(BF)

    return pl.pallas_call(
        kernel,
        out_shape=(
            jax.ShapeDtypeStruct((rows, heads_cols), BF),
            jax.ShapeDtypeStruct((rows, 2 * hd), BF),
        ),
        cost_estimate=estimate(4 * rows * width, 6 * rows * width),
        name="turn",
    )(summed, cosine, sine)


def attend(q, kv, places, own_place, state, diagonal):
    rows, cols = q.shape
    hd = kv.shape[2] // 2
    heads = cols // hd
    each = kv.shape[1] // rows
    blocks = kv.shape[0] * each
    scale = LOG2E / math.sqrt(hd)
    first = state is None

    def kernel(place_ref, own_ref, q_ref, kv_ref, *rest):
        if first:
            m_ref, l_ref, a_ref = rest
        else:
            m_in, l_in, a_in, m_ref, l_ref, a_ref = rest
        j = pl.program_id(0)

        @pl.when(j == 0)
        def _():
            if first:
                m_ref[...] = jnp.full(m_ref.shape, -1e30, F32)
                l_ref[...] = jnp.zeros(l_ref.shape, F32)
                a_ref[...] = jnp.zeros(a_ref.shape, F32)
            else:
                m_ref[...] = m_in[...]
                l_ref[...] = l_in[...]
                a_ref[...] = a_in[...]

        def block(masked):
            k = kv_ref[:, :hd]
            v = kv_ref[:, hd:]
            for h in range(heads):
                span = slice(h * hd, (h + 1) * hd)
                s = lax.dot_general(
                    q_ref[:, span], k, (((1,), (1,)), ((), ())), preferred_element_type=F32
                )
                if masked:
                    row = lax.broadcasted_iota(jnp.int32, s.shape, 0)
                    col = lax.broadcasted_iota(jnp.int32, s.shape, 1)
                    s = jnp.where(col <= row, s, -1e30)
                old = m_ref[:, span]
                new = jnp.maximum(old, jnp.max(s, axis=1, keepdims=True))
                alpha = jnp.exp2((old - new) * scale)
                pieces = []
                total = l_ref[:, span] * alpha
                for t in range(rows // hd):
                    p = jnp.exp2((s[:, t * hd : (t + 1) * hd] - new) * scale)
                    total = total + p
                    pieces.append(p.astype(BF))
                p = jnp.concatenate(pieces, axis=1)
                m_ref[:, span] = new
                l_ref[:, span] = total
                a_ref[:, span] = a_ref[:, span] * alpha + jnp.dot(
                    p, v, preferred_element_type=F32
                )

        if diagonal:
            block(True)
        else:

            @pl.when(place_ref[j] < own_ref[0])
            def _():
                block(False)

    full = pl.BlockSpec((rows, cols), lambda j, *_: (0, 0))
    shape = jax.ShapeDtypeStruct((rows, cols), F32)
    extra = () if first else state
    return pl.pallas_call(
        kernel,
        grid_spec=pltpu.PrefetchScalarGridSpec(
            num_scalar_prefetch=2,
            grid=(blocks,),
            in_specs=[full, pl.BlockSpec((None, rows, 2 * hd), lambda j, *_: (j // each, j % each, 0))]
            + [full] * len(extra),
            out_specs=(full, full, full),
        ),
        out_shape=(shape, shape, shape),
        compiler_params=params(),
        cost_estimate=estimate(
            4 * rows * rows * cols * blocks, 8 * rows * cols, rows * heads * rows * blocks
        ),
        name="attend",
    )(places, own_place, q, kv, *extra)


def close(state, hd):
    _, l, a = state
    rows, cols = a.shape

    def kernel(l_ref, a_ref, o_ref):
        for h in range(cols // hd):
            span = slice(h * hd, (h + 1) * hd)
            total = jnp.sum(l_ref[:, span], axis=1, keepdims=True)
            o_ref[:, span] = (a_ref[:, span] / total).astype(BF)

    return pl.pallas_call(
        kernel,
        out_shape=jax.ShapeDtypeStruct((rows, cols), BF),
        cost_estimate=estimate(2 * rows * cols, 10 * rows * cols),
        name="close",
    )(l, a)


def columns(x, w, tiles, width, addends, dtype):
    rows, depth = x.shape
    count = len(addends)
    steps = len(tiles)

    def kernel(where_ref, x_ref, w_ref, *rest):
        part = jnp.dot(x_ref[...], w_ref[...], preferred_element_type=F32)
        for a in rest[:count]:
            part = part + a[...].astype(F32)
        rest[count][...] = part.astype(dtype)

    piece = pl.BlockSpec((rows, width), lambda j, w: (0, j))
    return pl.pallas_call(
        kernel,
        grid_spec=pltpu.PrefetchScalarGridSpec(
            num_scalar_prefetch=1,
            grid=(steps,),
            in_specs=[
                pl.BlockSpec((rows, depth), lambda j, w: (0, 0)),
                pl.BlockSpec((depth, width), lambda j, w: (0, w[j])),
            ]
            + [piece] * count,
            out_specs=piece,
        ),
        out_shape=jax.ShapeDtypeStruct((rows, steps * width), dtype),
        compiler_params=params(),
        cost_estimate=estimate(2 * rows * depth * width * steps, 2 * depth * width * steps),
        name="columns",
    )(jnp.stack(tiles).astype(jnp.int32), x, w, *addends)


def body(
    tokens,
    query_weight,
    key_weight,
    value_weight,
    output_weight,
    key_cache,
    value_cache,
    cache_places,
    slab_places,
):
    rows = tokens.shape[0]
    hd = key_cache.shape[2]
    local_groups = key_cache.shape[1]
    nkey = lax.axis_size("key")
    nhid = lax.axis_size("hid")
    nhead = lax.axis_size("head")
    kid = lax.axis_index("key")
    hid = lax.axis_index("hid")
    head = lax.axis_index("head")
    core, far = hid % 2, hid // 2
    heads_cols = query_weight.shape[1] // nhid
    local_heads = heads_cols // hd
    group_heads = H // KVH

    def group_of(h):
        return (h * local_heads) // group_heads

    def to_core(a):
        return lax.ppermute(a, "hid", [(i, i ^ 1) for i in range(nhid)])

    def to_far(a):
        return lax.ppermute(a, "hid", [(i, i ^ 2) for i in range(nhid)])

    def to_head(a, m):
        return lax.ppermute(a, "head", [(i, i ^ m) for i in range(nhead)])

    group = group_of(hid)
    keys = lax.dynamic_slice_in_dim(key_cache, group, 1, 1)[:, 0]
    values = lax.dynamic_slice_in_dim(value_cache, group, 1, 1)[:, 0]
    own_kv = jnp.concatenate([keys, values], axis=1)

    half = own_kv.shape[0] // 2
    per = cache_places.shape[0] // 2
    low = (cache_places % 256).astype(BF)
    high = (cache_places // 256).astype(BF)
    tail = jnp.zeros((16, 2 * hd), BF).at[0, : 2 * per].set(low).at[1, : 2 * per].set(high)
    first = lax.all_gather(jnp.concatenate([own_kv[:half], tail], axis=0), "key")
    second = lax.all_gather(own_kv[half:], "key")
    codes = first[:, half : half + 2, : 2 * per].astype(jnp.int32)
    all_places = codes[:, 0] + 256 * codes[:, 1]
    mine = jnp.arange(nkey, dtype=jnp.int32)[:, None] == kid
    all_places = jnp.where(mine, FAR, all_places)

    own_place = lax.dynamic_slice_in_dim(slab_places, kid, 1, 0)
    spots = (own_place * rows + jnp.arange(rows, dtype=jnp.int32)).astype(F32)
    index = jnp.arange(hd // 2, dtype=F32)
    frequency = jnp.exp(index * (-2.0 * math.log(THETA) / hd))
    angles = spots[:, None] * frequency[None, :]
    cosine, sine = jnp.cos(angles), jnp.sin(angles)
    cosine = jnp.concatenate([cosine, cosine], axis=1)
    sine = jnp.concatenate([-sine, sine], axis=1)

    def proj(f, c, addends, dtype):
        d = f * 2 + c
        return project(
            tokens, query_weight, key_weight, value_weight, d, group_of(d), heads_cols,
            hd, addends, dtype,
        )

    p1 = to_core(proj(1 - far, 1 - core, (), BF))
    p3 = to_core(proj(far, 1 - core, (), BF))
    p2 = to_far(proj(1 - far, core, (p1,), BF))
    summed = proj(far, core, (p3, p2), F32)
    queries, fresh = turn(summed, cosine, sine, heads_cols)

    state = attend(queries, fresh[None], own_place, own_place, None, True)
    state = attend(queries, own_kv[None], cache_places, own_place, state, False)
    others, other_places = [], []
    for m in range(1, nkey):
        others.append(lax.ppermute(fresh, "key", [(i, (i + m) % nkey) for i in range(nkey)]))
        other_places.append(
            lax.dynamic_slice_in_dim(slab_places, (kid - m + nkey) % nkey, 1, 0)
        )
    state = attend(
        queries, jnp.concatenate(others, axis=0)[None], jnp.concatenate(other_places),
        own_place, state, False,
    )
    state = attend(queries, first, all_places[:, :per].reshape(-1), own_place, state, False)
    state = attend(queries, second, all_places[:, per:].reshape(-1), own_place, state, False)
    mixed = close(state, hd)

    block = output_weight.shape[1] // (nhead * nhid)
    wide = block // 2

    def tile(h, f, c, part):
        return (h * nhid + f * 2 + c) * 2 + part

    def mm(spots, part, addends, dtype):
        return columns(
            mixed, output_weight, [tile(h, f, c, part) for h, f, c in spots], wide, addends, dtype
        )

    every = [head ^ m for m in range(nhead)]
    a1 = to_core(mm([(h, 1 - far, 1 - core) for h in every], 0, (), BF))
    b1 = to_core(
        mm([(h, f, 1 - core) for h in every[1:] for f in (far, 1 - far)], 1, (), BF)
    )
    a2 = to_far(mm([(h, 1 - far, core) for h in every], 0, (a1,), BF))
    b2 = mm([(h, f, core) for h in every[1:] for f in (far, 1 - far)], 1, (b1,), BF)
    b2 = [
        to_head(b2[:, (m - 1) * 2 * wide : m * 2 * wide], m) for m in range(1, nhead)
    ]
    a3 = to_core(mm([(h, far, 1 - core) for h in every], 0, (), BF))
    b3 = to_core(mm([(head, f, 1 - core) for f in (far, 1 - far)], 1, (), BF))
    a4 = mm([(h, far, core) for h in every[1:]], 0, (a3[:, wide:], a2[:, wide:]), BF)
    a4 = [to_head(a4[:, (m - 1) * wide : m * wide], m) for m in range(1, nhead)]
    b4 = mm(
        [(head, 1 - far, core)], 1, (b3[:, wide:],) + tuple(b[:, wide:] for b in b2), BF
    )
    b4 = to_far(b4)
    a5 = mm([(head, far, core)], 0, (a3[:, :wide], a2[:, :wide]) + tuple(a4), BF)
    b5 = mm([(head, far, core)], 1, (b3[:, :wide],) + tuple(b[:, :wide] for b in b2) + (b4,), BF)
    return jnp.concatenate([a5, b5], axis=1)


def solution(mesh):
    return jax.shard_map(
        body,
        mesh=mesh,
        in_specs=(
            P("key", "hid"),
            P("hid", "head"),
            P("hid", "head"),
            P("hid", "head"),
            P(("head", "hid"), None),
            P("key", "head", None),
            P("key", "head", None),
            P("key"),
            P(),
        ),
        out_specs=P("key", ("head", "hid")),
        check_vma=False,
    )
```
